32 devices in a mesh: slab: 2 (over y), pencil: 16 (over z, x, core).
Axes of the slice: x: 2, y: 2, z: 4, core: 2. Of those that a mesh axis runs over, the one named last changes fastest.
Arguments:
- concentration: float32 [512, 512, 256], P('slab', 'pencil'), may hold values from -2 to 2.8
Outputs:
- updated: float32 [512, 512, 256], P('slab', 'pencil')
- mass: float32 [], replicated
The draws below stay inside these ranges and needn't reach their ends.
All inputs are finite; a program needn't handle non-finite values.
Results may differ from the reference program's by a relative error of at most 0.0002.
Values sent between devices are 32-bit elements; how exact they have to be, the bound alone decides.
No kernel may reach another device: no remote copies, remote signals or barrier semaphores. Data moves between devices by JAX's collectives and lax.ppermute only.
A program may use at most 128 MiB of HBM per device.

```python
import math
import jax
import jax.numpy as jnp

NX = 512
NY = 512
NZ = 256


def draw_concentration(key, part):
    noise_key = jax.random.fold_in(key, 11)
    phase_key = jax.random.fold_in(key, 23)
    first = jnp.arange(NX, dtype=jnp.float32)[:, None, None] / NX
    second = jnp.arange(NY, dtype=jnp.float32)[None, :, None] / NY
    third = jnp.arange(NZ, dtype=jnp.float32)[None, None, :] / NZ
    profile = 0.1 + 0.2 * first + 0.5 * second
    parity = jnp.arange(NX, dtype=jnp.int32) % 2
    alternate = jnp.where(parity == 0, 1.0, -1.0).astype(jnp.float32)[:, None, None]
    phases = jax.random.uniform(phase_key, (4,), jnp.float32, 0.0, 2.0 * math.pi)
    envelope = 0.75 + 0.125 * jnp.sin(2.0 * math.pi * second + phases[2]) + 0.125 * jnp.cos(2.0 * math.pi * third + phases[3])
    noise = 0.2 * jnp.clip(jax.random.normal(noise_key, (NX, NY, NZ), jnp.float32), -2.5, 2.5)
    return (profile + 1.5 * envelope * alternate + noise).astype(jnp.float32)


def setup_inputs(seed: int = 0) -> dict:
    streams_of = jax.random.split(jax.random.key(seed), 2)
    return {
        "concentration": draw_concentration(jax.random.fold_in(streams_of[1], 71), 0),
    }


time_step = 1.0
stiffness = 1.0


def wavenumber(length):
    index = jnp.arange(length, dtype=jnp.int32)
    signed = jnp.where(index < length // 2, index, index - length)
    return (2.0 * math.pi / length) * signed.astype(jnp.float32)


def reference(concentration):
    cube = concentration * concentration * concentration
    conc_hat = jnp.fft.fftn(concentration)
    cube_hat = jnp.fft.fftn(cube)
    wave_first = wavenumber(NX)
    wave_second = wavenumber(NY)
    wave_third = wavenumber(NZ)
    wave_square = wave_first[:, None, None] ** 2 + wave_second[None, :, None] ** 2 + wave_third[None, None, :] ** 2
    keep = jnp.where(jnp.arange(NZ, dtype=jnp.int32) == NZ // 2, 0.0, 1.0)[None, None, :]
    divisor = 1.0 + time_step * stiffness * wave_square * wave_square
    retain = keep * (1.0 + time_step * wave_square) / divisor
    forcing = keep * (time_step * wave_square) / divisor
    next_hat = retain * conc_hat - forcing * cube_hat
    updated = jnp.real(jnp.fft.ifftn(next_hat)).astype(concentration.dtype)
    mass = jnp.sum(concentration) / (NX * NY * NZ)
    return updated, mass
```

```python
import functools
import math

import jax
import jax.numpy as jnp
import numpy as np
from jax import lax
from jax.experimental import pallas as pl
from jax.experimental.pallas import tpu as pltpu
from jax.sharding import PartitionSpec as P

time_step = 1.0
stiffness = 1.0
VMEM_LIMIT = 60 * 1024 * 1024
LANES = 128


def split_table(table):
    high = table.astype(np.float32).astype(jnp.bfloat16)
    low = (table - high.astype(np.float64)).astype(np.float32).astype(jnp.bfloat16)
    return jnp.asarray(np.stack([high, low]))


def angles(rows, columns, length):
    return 2.0 * np.pi / length * ((rows[:, None] * columns[None, :]) % length)


def half_tables(length):
    half = length // 2
    cell = np.arange(half)
    forward_left, forward_right, inverse_left, inverse_right = [], [], [], []
    for parity in range(2):
        angle = angles(2 * cell + parity, cell, length)
        cos, sin = np.cos(angle), np.sin(angle)
        forward_left.append(np.block([[cos, sin], [-sin, cos]]))
        forward_right.append(np.block([[cos.T, -sin.T], [sin.T, cos.T]]))
        inverse_left.append(np.block([[cos.T, -sin.T], [sin.T, cos.T]]))
        inverse_right.append(np.block([[cos, sin], [-sin, cos]]))
    return tuple(
        split_table(np.stack(t)) for t in (forward_left, forward_right, inverse_left, inverse_right)
    )


def split(value):
    high = value.astype(jnp.bfloat16)
    low = (value - high.astype(jnp.float32)).astype(jnp.bfloat16)
    return high, low


def dot3(left, right, dims=((1,), (0,))):
    dot = functools.partial(
        lax.dot_general, dimension_numbers=(dims, ((), ())), preferred_element_type=jnp.float32
    )
    return dot(left[0], right[0]) + (dot(left[0], right[1]) + dot(left[1], right[0]))


def depth_forward(field, table, chunks, devices):
    first, second, depth = field.shape
    per_chunk = table.shape[1] // chunks
    pieces = depth // LANES

    def kernel(*refs):
        field_refs, table_ref, out_refs = refs[:pieces], refs[pieces], refs[pieces + 1 :]
        weights = (table_ref[0], table_ref[1])

        def body(row, _):
            conc = jnp.concatenate(
                [ref.reshape(LANES * 8, LANES)[pl.ds(row, LANES, stride=8), :] for ref in field_refs],
                axis=1,
            )
            for which, value in enumerate((conc, conc * conc * conc)):
                result = dot3(weights, split(value), ((1,), (1,)))
                for chunk in range(chunks):
                    rows_out = out_refs[chunk].reshape(devices * 4 * 8, LANES)
                    for part in range(2):
                        start = chunk * per_chunk + part * devices
                        rows_out[pl.ds((2 * which + part) * 8 + row, devices, stride=32), :] = result[
                            start : start + devices
                        ]
            return 0

        lax.fori_loop(0, 8, body, 0)

    return pl.pallas_call(
        kernel,
        grid=(second // 8, first // LANES),
        in_specs=[
            pl.BlockSpec((LANES, 8, LANES), lambda i, j, k=k: (j, i, k)) for k in range(pieces)
        ]
        + [pl.BlockSpec(table.shape, lambda i, j: (0, 0, 0))],
        out_specs=[pl.BlockSpec((devices, 4, 8, LANES), lambda i, j: (0, 0, i, j))] * chunks,
        out_shape=[jax.ShapeDtypeStruct((devices, 4, second, first), jnp.float32)] * chunks,
        compiler_params=pltpu.CompilerParams(vmem_limit_bytes=VMEM_LIMIT),
        cost_estimate=pl.CostEstimate(
            flops=12 * first * second * depth * table.shape[1],
            bytes_accessed=12 * first * second * depth,
            transcendentals=0,
        ),
        name="depth_forward",
    )(*[field] * pieces, table)


def depth_inverse(parts, table):
    devices, _, second, first = parts[0].shape
    depth = table.shape[2]

    def kernel(*refs):
        part_refs, table_ref, out_ref = refs[:-2], refs[-2], refs[-1]
        rows_out = out_ref.reshape(LANES * 8, LANES)
        weights = (table_ref[0], table_ref[1])

        def body(row, _):
            lines = jnp.concatenate(
                [
                    ref.reshape(devices * 2 * 8, LANES)[pl.ds(row, devices * 2, stride=8), :]
                    for ref in part_refs
                ],
                axis=0,
            )
            rows_out[pl.ds(row, LANES, stride=8), :] = dot3(split(lines), weights, ((0,), (0,)))
            return 0

        lax.fori_loop(0, 8, body, 0)

    return pl.pallas_call(
        kernel,
        grid=(second // 8, first // LANES, depth // LANES),
        in_specs=[pl.BlockSpec((devices, 2, 8, LANES), lambda i, j, k: (0, 0, i, j))] * len(parts)
        + [pl.BlockSpec((2, table.shape[1], LANES), lambda i, j, k: (0, 0, k))],
        out_specs=pl.BlockSpec((LANES, 8, LANES), lambda i, j, k: (j, i, k)),
        out_shape=jax.ShapeDtypeStruct((first, second, depth), jnp.float32),
        compiler_params=pltpu.CompilerParams(vmem_limit_bytes=VMEM_LIMIT),
        cost_estimate=pl.CostEstimate(
            flops=6 * first * second * depth * table.shape[1],
            bytes_accessed=8 * first * second * depth,
            transcendentals=0,
        ),
        name="depth_inverse",
    )(*parts, table)


def plane_step(lines, depth_index, waves, tables_first, tables_second, scale):
    slabs, pencils, _, second, first = lines.shape
    rows, columns = pencils * second // 2, first
    wave_first, wave_second, wave_third = waves

    def kernel(index_ref, third_ref, lines_ref, wf_ref, ws_ref, fr_ref, fl_ref, il_ref, ir_ref, out_ref, mid_ref, back_ref):
        def whole(slab, part):
            return lines_ref[slab, :, part].reshape(2 * rows, columns)

        for which in range(2):
            for parity in range(2):
                joined = []
                for part in range(2):
                    one, two = whole(0, 2 * which + part), whole(1, 2 * which + part)
                    joined.append(one + two if parity == 0 else one - two)
                result = dot3(
                    split(jnp.concatenate(joined, axis=1)), (fr_ref[0, parity], fr_ref[1, parity])
                )
                mid_ref[which, parity] = result
        third = third_ref[index_ref[0]]
        for parity in range(2):
            for parity_second in range(2):
                spectra = []
                for which in range(2):
                    top = mid_ref[which, parity, :rows]
                    bottom = mid_ref[which, parity, rows:]
                    both = top + bottom if parity_second == 0 else top - bottom
                    stacked = jnp.concatenate([both[:, :columns], both[:, columns:]], axis=0)
                    spectra.append(
                        dot3((fl_ref[0, parity_second], fl_ref[1, parity_second]), split(stacked))
                    )
                wave_square = wf_ref[parity][None, :] + ws_ref[parity_second] + third
                divisor = 1.0 + time_step * stiffness * wave_square * wave_square
                retain = scale * (1.0 + time_step * wave_square) / divisor
                forcing = scale * (time_step * wave_square) / divisor
                fresh = jnp.concatenate(
                    [
                        retain * spectra[0][:rows] - forcing * spectra[1][:rows],
                        retain * spectra[0][rows:] - forcing * spectra[1][rows:],
                    ],
                    axis=0,
                )
                result = dot3((il_ref[0, parity_second], il_ref[1, parity_second]), split(fresh))
                back_ref[parity_second] = jnp.concatenate([result[:rows], result[rows:]], axis=1)
            mid_ref[0, parity, :rows] = back_ref[0] + back_ref[1]
            mid_ref[0, parity, rows:] = back_ref[0] - back_ref[1]
        for parity in range(2):
            mid_ref[1, parity] = dot3(split(mid_ref[0, parity]), (ir_ref[0, parity], ir_ref[1, parity]))
        for part in range(2):
            span = slice(part * columns, (part + 1) * columns)
            even, odd = mid_ref[1, 0, :, span], mid_ref[1, 1, :, span]
            out_ref[0, :, part] = (even + odd).reshape(pencils, second, first)
            out_ref[1, :, part] = (even - odd).reshape(pencils, second, first)

    vmem = pl.BlockSpec(memory_space=pltpu.VMEM)
    smem = pl.BlockSpec(memory_space=pltpu.SMEM)
    forward_left, _, inverse_left, _ = tables_second
    _, forward_right, _, inverse_right = tables_first
    work = 2 * rows * columns * (2 * columns + 2 * rows) * 12 * 6
    return pl.pallas_call(
        kernel,
        in_specs=[smem, smem] + [vmem] * 7,
        out_specs=vmem,
        out_shape=jax.ShapeDtypeStruct((slabs, pencils, 2, second, first), jnp.float32),
        scratch_shapes=[
            pltpu.VMEM((2, 2, 2 * rows, 2 * columns), jnp.float32),
            pltpu.VMEM((2, rows, 2 * columns), jnp.float32),
        ],
        compiler_params=pltpu.CompilerParams(vmem_limit_bytes=VMEM_LIMIT),
        cost_estimate=pl.CostEstimate(
            flops=work, bytes_accessed=6 * lines.size, transcendentals=0
        ),
        name="plane_step",
    )(depth_index, wave_third, lines, wave_first, wave_second, forward_right, forward_left, inverse_left, inverse_right)


def wave_squares(length):
    index = np.arange(length)
    signed = np.where(index < length // 2, index, index - length).astype(np.float32)
    return np.square(np.float32(2.0 * math.pi / length) * signed)


def local(concentration, slabs, pencils):
    devices = slabs * pencils
    first, second, depth = concentration.shape
    total_first, total_second = first * slabs, second * pencils
    kept = depth // 2
    chunks = kept // devices
    tables_first, tables_second = half_tables(total_first), half_tables(total_second)

    index = np.arange(kept).reshape(chunks, devices)
    angle = angles(index.reshape(-1), np.arange(depth), depth).reshape(chunks, devices, depth)
    forward = np.stack([np.cos(angle), -np.sin(angle)], axis=1).reshape(2 * kept, depth)
    weights = np.where(index == 0, 1.0, 2.0)[:, :, None]
    inverse = np.stack([weights * np.cos(angle), -weights * np.sin(angle)], axis=2)
    inverse = inverse.reshape(2 * kept, depth)

    parity_waves_first = jnp.asarray(wave_squares(total_first).reshape(-1, 2).T)
    parity_waves_second = jnp.asarray(wave_squares(total_second).reshape(-1, 2).T[:, :, None])
    third = jnp.asarray(wave_squares(depth)[:kept])
    waves = (parity_waves_first, parity_waves_second, third)
    me = lax.axis_index(("slab", "pencil"))
    scale = 1.0 / (total_first * total_second * depth)

    sent = depth_forward(concentration, split_table(forward), chunks, devices)
    back = []
    for chunk in range(chunks):
        lines = lax.all_to_all(sent[chunk], ("slab", "pencil"), split_axis=0, concat_axis=0, tiled=True)
        lines = lines.reshape(slabs, pencils, 4, second, first)
        fresh = plane_step(
            lines, (chunk * devices + me).reshape(1), waves, tables_first, tables_second, scale
        ).reshape(devices, 2, second, first)
        back.append(lax.all_to_all(fresh, ("slab", "pencil"), split_axis=0, concat_axis=0, tiled=True))
    updated = depth_inverse(back, split_table(inverse))
    mass = lax.psum(jnp.sum(concentration), ("slab", "pencil")) * scale
    return updated, mass


def solution(mesh):
    sizes = dict(mesh.shape)
    return jax.shard_map(
        functools.partial(local, slabs=sizes["slab"], pencils=sizes["pencil"]),
        mesh=mesh,
        in_specs=(P("slab", "pencil", None),),
        out_specs=(P("slab", "pencil", None), P()),
        check_vma=False,
    )
```

```python
import functools
import math

import jax
import jax.numpy as jnp
import numpy as np
from jax import lax
from jax.experimental import pallas as pl
from jax.experimental.pallas import tpu as pltpu
from jax.sharding import Mesh
from jax.sharding import PartitionSpec as P


time_step = 1.0
stiffness = 1.0
VMEM_LIMIT = 60 * 1024 * 1024
LANES = 128
CHUNKS = [2, 2, 2, 2]


def split_table(table):
    high = table.astype(np.float32).astype(jnp.bfloat16)
    low = (table - high.astype(np.float64)).astype(np.float32).astype(jnp.bfloat16)
    return jnp.asarray(np.stack([high, low]))


def angles(rows, columns, length):
    return 2.0 * np.pi / length * ((rows[:, None] * columns[None, :]) % length)


def half_tables(length):
    half = length // 2
    cell = np.arange(half)
    forward_left, forward_right, inverse_left, inverse_right = [], [], [], []
    for parity in range(2):
        angle = angles(2 * cell + parity, cell, length)
        cos, sin = np.cos(angle), np.sin(angle)
        forward_left.append(np.block([[cos, sin], [-sin, cos]]))
        forward_right.append(np.block([[cos.T, -sin.T], [sin.T, cos.T]]))
        inverse_left.append(np.block([[cos.T, -sin.T], [sin.T, cos.T]]))
        inverse_right.append(np.block([[cos, sin], [-sin, cos]]))
    return tuple(
        split_table(np.stack(t)) for t in (forward_left, forward_right, inverse_left, inverse_right)
    )


def split(value):
    high = value.astype(jnp.bfloat16)
    low = (value - high.astype(jnp.float32)).astype(jnp.bfloat16)
    return high, low


def dot3(left, right, dims=((1,), (0,))):
    dot = functools.partial(
        lax.dot_general, dimension_numbers=(dims, ((), ())), preferred_element_type=jnp.float32
    )
    return dot(left[0], right[0]) + (dot(left[0], right[1]) + dot(left[1], right[0]))


def depth_forward(field, table, counts, devices):
    first, second, depth = field.shape
    pieces = depth // LANES
    shapes = [(devices, count, 4, second, first) for count in counts]

    def kernel(*refs):
        field_refs, table_ref, out_refs = refs[:pieces], refs[pieces], refs[pieces + 1 :]
        weights = (table_ref[0], table_ref[1])

        def body(row, _):
            conc = jnp.concatenate(
                [
                    ref.reshape(LANES * 8, LANES)[pl.ds(row, LANES, stride=8), :].T
                    for ref in field_refs
                ],
                axis=0,
            )
            for which, value in enumerate((conc, conc * conc * conc)):
                result = dot3(weights, split(value))
                start = 0
                for count, out_ref in zip(counts, out_refs):
                    rows_out = out_ref.reshape(devices * count * 4 * 8, LANES)
                    for index in range(count):
                        for part in range(2):
                            place = (index * 4 + 2 * which + part) * 8 + row
                            rows_out[pl.ds(place, devices, stride=count * 32), :] = result[
                                start : start + devices
                            ]
                            start += devices
            return 0

        lax.fori_loop(0, 8, body, 0, unroll=8)

    return pl.pallas_call(
        kernel,
        grid=(second // 8, first // LANES),
        in_specs=[
            pl.BlockSpec((LANES, 8, LANES), lambda i, j, k=k: (j, i, k)) for k in range(pieces)
        ]
        + [pl.BlockSpec(table.shape, lambda i, j: (0, 0, 0))],
        out_specs=[pl.BlockSpec((*s[:3], 8, LANES), lambda i, j: (0, 0, 0, i, j)) for s in shapes],
        out_shape=[jax.ShapeDtypeStruct(s, jnp.float32) for s in shapes],
        compiler_params=pltpu.CompilerParams(vmem_limit_bytes=VMEM_LIMIT),
        cost_estimate=pl.CostEstimate(
            flops=12 * first * second * depth * table.shape[1],
            bytes_accessed=4 * first * second * (depth + 2 * table.shape[1]),
            transcendentals=0,
        ),
        name="depth_forward",
    )(*[field] * pieces, table)


def depth_inverse(parts, table, before=None):
    devices, _, _, second, first = parts[0].shape
    counts = [part.shape[1] for part in parts]
    depth = table.shape[2]
    last = before is not None
    width = LANES if last else depth

    def kernel(*refs):
        part_refs, table_ref, out_ref = refs[: len(parts)], refs[len(parts)], refs[-1]
        weights = (table_ref[0], table_ref[1])

        def body(row, _):
            lines = jnp.concatenate(
                [
                    ref.reshape(devices * count * 2 * 8, LANES)[
                        pl.ds(row, devices * count * 2, stride=8), :
                    ]
                    for ref, count in zip(part_refs, counts)
                ],
                axis=0,
            )
            result = dot3(split(lines.T), weights)
            if last:
                out_ref.reshape(LANES * 8, LANES)[pl.ds(row, LANES, stride=8), :] = result + refs[-2][row]
            else:
                out_ref[row] = result
            return 0

        lax.fori_loop(0, 8, body, 0, unroll=8)

    by_second = pl.BlockSpec((8, LANES, width), lambda i, j, k: (i, j, k))
    by_first = pl.BlockSpec((LANES, 8, width), lambda i, j, k: (j, i, k))
    out = (first, second, depth) if last else (second, first, depth)
    return pl.pallas_call(
        kernel,
        grid=(second // 8, first // LANES, depth // width),
        in_specs=[
            pl.BlockSpec((devices, count, 2, 8, LANES), lambda i, j, k: (0, 0, 0, i, j))
            for count in counts
        ]
        + [pl.BlockSpec((2, table.shape[1], width), lambda i, j, k: (0, 0, k))]
        + [by_second] * last,
        out_specs=by_first if last else by_second,
        out_shape=jax.ShapeDtypeStruct(out, jnp.float32),
        compiler_params=pltpu.CompilerParams(vmem_limit_bytes=VMEM_LIMIT),
        cost_estimate=pl.CostEstimate(
            flops=6 * first * second * depth * table.shape[1],
            bytes_accessed=4 * first * second * (depth * (1 + last) + table.shape[1]),
            transcendentals=0,
        ),
        name="depth_inverse",
    )(*parts, table, *([before] if last else []))


def plane_forward(lines, depth_index, waves, tables_first, tables_second, scale):
    slabs, others, count, _, second, first = lines.shape
    rows, columns = others * second, first
    wave_first, wave_second, wave_third = waves

    def kernel(index_ref, third_ref, lines_ref, wf_ref, ws_ref, fr_ref, fl_ref, il_ref, own_ref, other_ref, mid_ref):
        third_index = index_ref[0] + pl.program_id(0) * index_ref[1]
        carries = jnp.where(third_index == 0, 0.0, 1.0)
        for which in range(2):
            for parity in range(2):
                joined = []
                for part in range(2):
                    one, two = (
                        lines_ref[slab, :, 0, 2 * which + part].reshape(rows, columns) for slab in range(2)
                    )
                    value = one + two if parity == 0 else one - two
                    joined.append(value * carries if (which, part) == (0, 1) else value)
                result = dot3(
                    split(jnp.concatenate(joined, axis=1)), (fr_ref[0, parity], fr_ref[1, parity])
                )
                mid_ref[which, parity, :rows] = result[:, :columns]
                mid_ref[which, parity, rows:] = result[:, columns:]
        third = third_ref[third_index]
        for parity in range(2):
            stacked = [split(mid_ref[which, parity]) for which in range(2)]
            back = []
            for parity_second in range(2):
                table = (fl_ref[0, parity_second], fl_ref[1, parity_second])
                spectra = [dot3(table, stacked[which]) for which in range(2)]
                wave_square = wf_ref[parity][None, :] + ws_ref[parity_second] + third
                divisor = 1.0 + time_step * stiffness * wave_square * wave_square
                retain = scale * (1.0 + time_step * wave_square) / divisor
                forcing = scale * (time_step * wave_square) / divisor
                fresh = jnp.concatenate(
                    [
                        retain * spectra[0][:rows] - forcing * spectra[1][:rows],
                        retain * spectra[0][rows:] - forcing * spectra[1][rows:],
                    ],
                    axis=0,
                )
                back.append(dot3((il_ref[0, parity_second], il_ref[1, parity_second]), split(fresh)))
            for out_ref, value in ((own_ref, back[0] + back[1]), (other_ref, back[0] - back[1])):
                out_ref[0, parity, :, :columns] = value[:rows]
                out_ref[0, parity, :, columns:] = value[rows:]

    smem = pl.BlockSpec(memory_space=pltpu.SMEM)
    fixed = lambda a: pl.BlockSpec(a.shape, lambda i: (0,) * a.ndim)
    forward_left, _, inverse_left, _ = tables_second
    _, forward_right, _, _ = tables_first
    consts = (wave_first, wave_second, forward_right, forward_left, inverse_left)
    out = (count, 2, rows, 2 * columns)
    return pl.pallas_call(
        kernel,
        grid=(count,),
        in_specs=[smem, smem, pl.BlockSpec((slabs, others, 1, 4, second, first), lambda i: (0, 0, i, 0, 0, 0))]
        + [fixed(a) for a in consts],
        out_specs=[pl.BlockSpec((1, *out[1:]), lambda i: (i, 0, 0, 0))] * 2,
        out_shape=[jax.ShapeDtypeStruct(out, jnp.float32)] * 2,
        scratch_shapes=[pltpu.VMEM((2, 2, 2 * rows, columns), jnp.float32)],
        compiler_params=pltpu.CompilerParams(vmem_limit_bytes=VMEM_LIMIT),
        cost_estimate=pl.CostEstimate(
            flops=count * 6 * 4 * rows * columns * (4 * columns + 12 * rows),
            bytes_accessed=8 * lines.size,
            transcendentals=0,
        ),
        name="plane_forward",
    )(depth_index, wave_third, lines, *consts)


def plane_inverse(own, near, far, tables_first, second):
    count, _, rows, columns = own.shape
    columns //= 2
    others = rows // second

    def kernel(own_ref, near_ref, far_ref, ir_ref, out_ref):
        even, odd = (
            dot3(split(own_ref[0, p] + (near_ref[0, p] + far_ref[0, p])), (ir_ref[0, p], ir_ref[1, p]))
            for p in range(2)
        )
        for slab, value in enumerate((even + odd, even - odd)):
            for part in range(2):
                span = slice(part * columns, (part + 1) * columns)
                out_ref[slab, :, 0, part] = value[:, span].reshape(others, second, columns)

    table = tables_first[3]
    spec = pl.BlockSpec((1, *own.shape[1:]), lambda i: (i, 0, 0, 0))
    return pl.pallas_call(
        kernel,
        grid=(count,),
        in_specs=[spec, spec, spec, pl.BlockSpec(table.shape, lambda i: (0, 0, 0, 0))],
        out_specs=pl.BlockSpec((2, others, 1, 2, second, columns), lambda i: (0, 0, i, 0, 0, 0)),
        out_shape=jax.ShapeDtypeStruct((2, others, count, 2, second, columns), jnp.float32),
        compiler_params=pltpu.CompilerParams(vmem_limit_bytes=VMEM_LIMIT),
        cost_estimate=pl.CostEstimate(
            flops=count * 6 * 4 * rows * columns * 2 * columns,
            bytes_accessed=12 * own.size,
            transcendentals=0,
        ),
        name="plane_inverse",
    )(own, near, far, table)


def wave_squares(length):
    index = np.arange(length)
    signed = np.where(index < length // 2, index, index - length).astype(np.float32)
    return np.square(np.float32(2.0 * math.pi / length) * signed)


def chunk_counts(total):
    return CHUNKS if sum(CHUNKS) == total else [1] * total


def local(concentration, slabs, others):
    devices = slabs * others
    first, second, depth = concentration.shape
    total_first, total_second = first * slabs, 2 * second * others
    kept = depth // 2
    counts = chunk_counts(kept // devices)
    zero_chunk = min(1, len(counts) - 1)
    starts = [0] * len(counts)
    for chunk in range(len(counts)):
        if chunk != zero_chunk:
            starts[chunk] = counts[zero_chunk] + sum(
                counts[c] for c in range(chunk) if c != zero_chunk
            )
    tables_first, tables_second = half_tables(total_first), half_tables(total_second)

    mirrored = np.arange(devices) ^ (others // 2)

    def by_half(rows, axis):
        return np.stack([r.reshape(-1, depth) for r in (rows, np.take(rows, mirrored, axis))])

    half = lax.axis_index("half")

    def table_of(pair):
        return lax.dynamic_index_in_dim(split_table(pair), half, 1, keepdims=False)

    forward, inverse = [], []
    for start, count in zip(starts, counts):
        index = np.arange(start * devices, (start + count) * devices)
        angle = angles(index, np.arange(depth), depth).reshape(count, devices, depth)
        forward.append(by_half(np.stack([np.cos(angle), -np.sin(angle)], axis=1), 2))
        weights = np.where(index == 0, 1.0, 2.0).reshape(count, devices, 1)
        waves = np.stack([weights * np.cos(angle), -weights * np.sin(angle)], axis=2)
        inverse.append(by_half(waves.transpose(1, 0, 2, 3), 0))

    parity_waves_first = jnp.asarray(wave_squares(total_first).reshape(-1, 2).T)
    parity_waves_second = jnp.asarray(wave_squares(total_second).reshape(-1, 2).T[:, :, None])
    third = jnp.asarray(wave_squares(depth)[:kept])
    waves = (parity_waves_first, parity_waves_second, third)
    group = ("slab", "other")
    me = lax.axis_index(group) ^ (half * (others // 2))
    scale = 1.0 / (total_first * total_second * depth)

    partners = [(i, others + (i ^ (others // 2))) for i in range(others)]
    both_ways = [((a, b), (b, a)) for a, b in partners]
    far_pairs = [pair for way in both_ways[: others // 2] for pair in way]
    near_pairs = [pair for way in both_ways[others // 2 :] for pair in way]

    def exchange(value):
        return lax.all_to_all(value, group, split_axis=0, concat_axis=0, tiled=True)

    sent = depth_forward(concentration, table_of(forward[0]), counts[:1], devices)
    sent += depth_forward(
        concentration, table_of(np.concatenate(forward[1:], axis=1)), counts[1:], devices
    )
    sent = list(sent)
    is_zero, zero_place = me == 0, half * (others // 2)
    mass = jnp.sum(concentration)
    sent[zero_chunk] = sent[zero_chunk].at[zero_place, 0, 1, 0, 0].set(mass)
    back = []
    for chunk, count in enumerate(counts):
        lines = exchange(sent[chunk])
        lines = lines.reshape(slabs, others, count, 4, second, first)
        if chunk == zero_chunk:
            mass = jnp.sum(lines[:, :, 0, 1, 0, 0])
        index = jnp.stack([starts[chunk] * devices + me, jnp.int32(devices)])
        own, other = plane_forward(lines, index, waves, tables_first, tables_second, scale)
        if chunk == zero_chunk:
            spot = (0, 0, 0, first)
            other = other.at[spot].set(jnp.where(is_zero, mass, other[spot]))
        near = lax.ppermute(other, ("half", "other"), near_pairs)
        far = lax.ppermute(other, ("half", "other"), far_pairs)
        if chunk == zero_chunk:
            mass += near[spot] + far[spot]
            near = near.at[spot].set(jnp.where(is_zero, 0.0, near[spot]))
            far = far.at[spot].set(jnp.where(is_zero, 0.0, far[spot]))
        fresh = plane_inverse(own, near, far, tables_first, second)
        if chunk == zero_chunk:
            spot = (slice(None), slice(None), 0, 1, 0, 0)
            fresh = fresh.at[spot].set(jnp.where(is_zero, mass, fresh[spot]))
        back.append(exchange(fresh.reshape(devices, count, 2, second, first)))
    updated = depth_inverse(back[:-1], table_of(np.concatenate(inverse[:-1], axis=1)))
    updated = depth_inverse(back[-1:], table_of(inverse[-1]), updated)
    mass = back[zero_chunk][zero_place, 0, 1, 0, 0] * scale
    return updated, mass


def solution(mesh):
    slabs, pencils = mesh.shape["slab"], mesh.shape["pencil"]
    halves = Mesh(mesh.devices.reshape(slabs, 2, pencils // 2), ("slab", "half", "other"))
    field = P("slab", ("half", "other"), None)

    def body(concentration):
        return local(concentration, slabs, pencils // 2)

    return jax.shard_map(
        body, mesh=halves, in_specs=(field,), out_specs=(field, P()), check_vma=False
    )
```

```python
import functools
import math

import jax
import jax.numpy as jnp
import numpy as np
from jax import lax
from jax.experimental import pallas as pl
from jax.experimental.pallas import tpu as pltpu
from jax.sharding import Mesh
from jax.sharding import PartitionSpec as P


time_step = 1.0
stiffness = 1.0
VMEM_LIMIT = 60 * 1024 * 1024
LANES = 128
CHUNKS = [2, 2, 2, 2]


def split_table(table):
    high = table.astype(np.float32).astype(jnp.bfloat16)
    low = (table - high.astype(np.float64)).astype(np.float32).astype(jnp.bfloat16)
    return jnp.asarray(np.stack([high, low]))


def angles(rows, columns, length):
    return 2.0 * np.pi / length * ((rows[:, None] * columns[None, :]) % length)


def half_tables(length):
    half = length // 2
    cell = np.arange(half)
    forward_left, forward_right, inverse_left, inverse_right = [], [], [], []
    for parity in range(2):
        angle = angles(2 * cell + parity, cell, length)
        cos, sin = np.cos(angle), np.sin(angle)
        forward_left.append(np.block([[cos, sin], [-sin, cos]]))
        forward_right.append(np.block([[cos.T, -sin.T], [sin.T, cos.T]]))
        inverse_left.append(np.block([[cos.T, -sin.T], [sin.T, cos.T]]))
        inverse_right.append(np.block([[cos, sin], [-sin, cos]]))
    return tuple(
        split_table(np.stack(t)) for t in (forward_left, forward_right, inverse_left, inverse_right)
    )


def split(value):
    high = value.astype(jnp.bfloat16)
    low = (value - high.astype(jnp.float32)).astype(jnp.bfloat16)
    return high, low


def dot3(left, right, dims=((1,), (0,))):
    dot = functools.partial(
        lax.dot_general, dimension_numbers=(dims, ((), ())), preferred_element_type=jnp.float32
    )
    return dot(left[0], right[0]) + (dot(left[0], right[1]) + dot(left[1], right[0]))


def depth_forward(field, table, counts, devices):
    first, second, depth = field.shape
    pieces = depth // LANES
    shapes = [(devices, count, 4, second, first) for count in counts]

    def kernel(*refs):
        field_refs, table_ref, out_refs = refs[:pieces], refs[pieces], refs[pieces + 1 :]
        weights = (table_ref[0], table_ref[1])

        def body(row, _):
            conc = jnp.concatenate(
                [
                    ref.reshape(LANES * 8, LANES)[pl.ds(row, LANES, stride=8), :].T
                    for ref in field_refs
                ],
                axis=0,
            )
            for which, value in enumerate((conc, conc * conc * conc)):
                result = dot3(weights, split(value))
                start = 0
                for count, out_ref in zip(counts, out_refs):
                    rows_out = out_ref.reshape(devices * count * 4 * 8, LANES)
                    for index in range(count):
                        for part in range(2):
                            place = (index * 4 + 2 * which + part) * 8 + row
                            rows_out[pl.ds(place, devices, stride=count * 32), :] = result[
                                start : start + devices
                            ]
                            start += devices
            return 0

        lax.fori_loop(0, 8, body, 0, unroll=8)

    return pl.pallas_call(
        kernel,
        grid=(second // 8, first // LANES),
        in_specs=[
            pl.BlockSpec((LANES, 8, LANES), lambda i, j, k=k: (j, i, k)) for k in range(pieces)
        ]
        + [pl.BlockSpec(table.shape, lambda i, j: (0, 0, 0))],
        out_specs=[pl.BlockSpec((*s[:3], 8, LANES), lambda i, j: (0, 0, 0, i, j)) for s in shapes],
        out_shape=[jax.ShapeDtypeStruct(s, jnp.float32) for s in shapes],
        compiler_params=pltpu.CompilerParams(vmem_limit_bytes=VMEM_LIMIT),
        cost_estimate=pl.CostEstimate(
            flops=12 * first * second * depth * table.shape[1],
            bytes_accessed=4 * first * second * (depth + 2 * table.shape[1]),
            transcendentals=0,
        ),
        name="depth_forward",
    )(*[field] * pieces, table)


def depth_inverse(parts, table, before=None):
    devices, _, _, second, first = parts[0].shape
    counts = [part.shape[1] for part in parts]
    depth = table.shape[2]
    last = before is not None
    width = LANES if last else depth

    def kernel(*refs):
        part_refs, table_ref, out_ref = refs[: len(parts)], refs[len(parts)], refs[-1]
        weights = (table_ref[0], table_ref[1])

        def body(row, _):
            lines = jnp.concatenate(
                [
                    ref.reshape(devices * count * 2 * 8, LANES)[
                        pl.ds(row, devices * count * 2, stride=8), :
                    ]
                    for ref, count in zip(part_refs, counts)
                ],
                axis=0,
            )
            result = dot3(split(lines.T), weights)
            if last:
                out_ref.reshape(LANES * 8, LANES)[pl.ds(row, LANES, stride=8), :] = result + refs[-2][row]
            else:
                out_ref[row] = result
            return 0

        lax.fori_loop(0, 8, body, 0, unroll=8)

    by_second = pl.BlockSpec((8, LANES, width), lambda i, j, k: (i, j, k))
    by_first = pl.BlockSpec((LANES, 8, width), lambda i, j, k: (j, i, k))
    out = (first, second, depth) if last else (second, first, depth)
    return pl.pallas_call(
        kernel,
        grid=(second // 8, first // LANES, depth // width),
        in_specs=[
            pl.BlockSpec((devices, count, 2, 8, LANES), lambda i, j, k: (0, 0, 0, i, j))
            for count in counts
        ]
        + [pl.BlockSpec((2, table.shape[1], width), lambda i, j, k: (0, 0, k))]
        + [by_second] * last,
        out_specs=by_first if last else by_second,
        out_shape=jax.ShapeDtypeStruct(out, jnp.float32),
        compiler_params=pltpu.CompilerParams(vmem_limit_bytes=VMEM_LIMIT),
        cost_estimate=pl.CostEstimate(
            flops=6 * first * second * depth * table.shape[1],
            bytes_accessed=4 * first * second * (depth * (1 + last) + table.shape[1]),
            transcendentals=0,
        ),
        name="depth_inverse",
    )(*parts, table, *([before] if last else []))


def plane_forward(lines, depth_index, waves, tables_first, tables_second, scale):
    slabs, others, count, _, second, first = lines.shape
    rows, columns = others * second, first
    wave_first, wave_second, wave_third = waves

    def kernel(index_ref, third_ref, lines_ref, wf_ref, ws_ref, fr_ref, fl_ref, il_ref, own_ref, other_ref, mid_ref):
        third_index = index_ref[0] + pl.program_id(0) * index_ref[1]
        carries = jnp.where(third_index == 0, 0.0, 1.0)
        for which in range(2):
            for parity in range(2):
                joined = []
                for part in range(2):
                    one, two = (
                        lines_ref[slab, :, 0, 2 * which + part].reshape(rows, columns) for slab in range(2)
                    )
                    value = one + two if parity == 0 else one - two
                    joined.append(value * carries if (which, part) == (0, 1) else value)
                result = dot3(
                    split(jnp.concatenate(joined, axis=1)), (fr_ref[0, parity], fr_ref[1, parity])
                )
                mid_ref[which, parity, :rows] = result[:, :columns]
                mid_ref[which, parity, rows:] = result[:, columns:]
        third = third_ref[third_index]
        for parity in range(2):
            stacked = [split(mid_ref[which, parity]) for which in range(2)]
            back = []
            for parity_second in range(2):
                table = (fl_ref[0, parity_second], fl_ref[1, parity_second])
                spectra = [dot3(table, stacked[which]) for which in range(2)]
                wave_square = wf_ref[parity][None, :] + ws_ref[parity_second] + third
                divisor = 1.0 + time_step * stiffness * wave_square * wave_square
                retain = scale * (1.0 + time_step * wave_square) / divisor
                forcing = scale * (time_step * wave_square) / divisor
                fresh = jnp.concatenate(
                    [
                        retain * spectra[0][:rows] - forcing * spectra[1][:rows],
                        retain * spectra[0][rows:] - forcing * spectra[1][rows:],
                    ],
                    axis=0,
                )
                back.append(dot3((il_ref[0, parity_second], il_ref[1, parity_second]), split(fresh)))
            for out_ref, value in ((own_ref, back[0] + back[1]), (other_ref, back[0] - back[1])):
                out_ref[0, parity, :, :columns] = value[:rows]
                out_ref[0, parity, :, columns:] = value[rows:]

    smem = pl.BlockSpec(memory_space=pltpu.SMEM)
    fixed = lambda a: pl.BlockSpec(a.shape, lambda i: (0,) * a.ndim)
    forward_left, _, inverse_left, _ = tables_second
    _, forward_right, _, _ = tables_first
    consts = (wave_first, wave_second, forward_right, forward_left, inverse_left)
    out = (count, 2, rows, 2 * columns)
    return pl.pallas_call(
        kernel,
        grid=(count,),
        in_specs=[smem, smem, pl.BlockSpec((slabs, others, 1, 4, second, first), lambda i: (0, 0, i, 0, 0, 0))]
        + [fixed(a) for a in consts],
        out_specs=[pl.BlockSpec((1, *out[1:]), lambda i: (i, 0, 0, 0))] * 2,
        out_shape=[jax.ShapeDtypeStruct(out, jnp.float32)] * 2,
        scratch_shapes=[pltpu.VMEM((2, 2, 2 * rows, columns), jnp.float32)],
        compiler_params=pltpu.CompilerParams(vmem_limit_bytes=VMEM_LIMIT),
        cost_estimate=pl.CostEstimate(
            flops=count * 6 * 4 * rows * columns * (4 * columns + 12 * rows),
            bytes_accessed=8 * lines.size,
            transcendentals=0,
        ),
        name="plane_forward",
    )(depth_index, wave_third, lines, *consts)


def plane_inverse(own, other, tables_first, second):
    count, _, rows, columns = own.shape
    columns //= 2
    others = rows // second

    def kernel(own_ref, other_ref, ir_ref, out_ref):
        even, odd = (
            dot3(split(own_ref[0, p] + other_ref[0, p]), (ir_ref[0, p], ir_ref[1, p]))
            for p in range(2)
        )
        for slab, value in enumerate((even + odd, even - odd)):
            for part in range(2):
                span = slice(part * columns, (part + 1) * columns)
                out_ref[slab, :, 0, part] = value[:, span].reshape(others, second, columns)

    table = tables_first[3]
    spec = pl.BlockSpec((1, *own.shape[1:]), lambda i: (i, 0, 0, 0))
    return pl.pallas_call(
        kernel,
        grid=(count,),
        in_specs=[spec, spec, pl.BlockSpec(table.shape, lambda i: (0, 0, 0, 0))],
        out_specs=pl.BlockSpec((2, others, 1, 2, second, columns), lambda i: (0, 0, i, 0, 0, 0)),
        out_shape=jax.ShapeDtypeStruct((2, others, count, 2, second, columns), jnp.float32),
        compiler_params=pltpu.CompilerParams(vmem_limit_bytes=VMEM_LIMIT),
        cost_estimate=pl.CostEstimate(
            flops=count * 6 * 4 * rows * columns * 2 * columns,
            bytes_accessed=12 * own.size,
            transcendentals=0,
        ),
        name="plane_inverse",
    )(own, other, table)


def wave_squares(length):
    index = np.arange(length)
    signed = np.where(index < length // 2, index, index - length).astype(np.float32)
    return np.square(np.float32(2.0 * math.pi / length) * signed)


def chunk_counts(total):
    return CHUNKS if sum(CHUNKS) == total else [1] * total


def local(concentration, slabs, others):
    devices = slabs * others
    first, second, depth = concentration.shape
    total_first, total_second = first * slabs, 2 * second * others
    kept = depth // 2
    counts = chunk_counts(kept // devices)
    zero_chunk = min(1, len(counts) - 1)
    starts = [0] * len(counts)
    for chunk in range(len(counts)):
        if chunk != zero_chunk:
            starts[chunk] = counts[zero_chunk] + sum(
                counts[c] for c in range(chunk) if c != zero_chunk
            )
    tables_first, tables_second = half_tables(total_first), half_tables(total_second)

    mirrored = np.arange(devices) ^ (others // 2)

    def by_half(rows, axis):
        return np.stack([r.reshape(-1, depth) for r in (rows, np.take(rows, mirrored, axis))])

    half = lax.axis_index("half")

    def table_of(pair):
        return lax.dynamic_index_in_dim(split_table(pair), half, 1, keepdims=False)

    forward, inverse = [], []
    for start, count in zip(starts, counts):
        index = np.arange(start * devices, (start + count) * devices)
        angle = angles(index, np.arange(depth), depth).reshape(count, devices, depth)
        forward.append(by_half(np.stack([np.cos(angle), -np.sin(angle)], axis=1), 2))
        weights = np.where(index == 0, 1.0, 2.0).reshape(count, devices, 1)
        waves = np.stack([weights * np.cos(angle), -weights * np.sin(angle)], axis=2)
        inverse.append(by_half(waves.transpose(1, 0, 2, 3), 0))

    parity_waves_first = jnp.asarray(wave_squares(total_first).reshape(-1, 2).T)
    parity_waves_second = jnp.asarray(wave_squares(total_second).reshape(-1, 2).T[:, :, None])
    third = jnp.asarray(wave_squares(depth)[:kept])
    waves = (parity_waves_first, parity_waves_second, third)
    group = ("slab", "other")
    me = lax.axis_index(group) ^ (half * (others // 2))
    scale = 1.0 / (total_first * total_second * depth)

    partners = [(i, others + (i ^ (others // 2))) for i in range(others)]
    pairs = [pair for a, b in partners for pair in ((a, b), (b, a))]

    def exchange(value):
        return lax.all_to_all(value, group, split_axis=0, concat_axis=0, tiled=True)

    sent = depth_forward(concentration, table_of(forward[0]), counts[:1], devices)
    sent += depth_forward(
        concentration, table_of(np.concatenate(forward[1:], axis=1)), counts[1:], devices
    )
    sent = list(sent)
    is_zero, zero_place = me == 0, half * (others // 2)
    mass = jnp.sum(concentration)
    sent[zero_chunk] = sent[zero_chunk].at[zero_place, 0, 1, 0, 0].set(mass)
    back = []
    for chunk, count in enumerate(counts):
        lines = exchange(sent[chunk])
        lines = lines.reshape(slabs, others, count, 4, second, first)
        if chunk == zero_chunk:
            mass = jnp.sum(lines[:, :, 0, 1, 0, 0])
        index = jnp.stack([starts[chunk] * devices + me, jnp.int32(devices)])
        own, other = plane_forward(lines, index, waves, tables_first, tables_second, scale)
        if chunk == zero_chunk:
            spot = (0, 0, 0, first)
            other = other.at[spot].set(jnp.where(is_zero, mass, other[spot]))
        other = lax.ppermute(other, ("half", "other"), pairs)
        if chunk == zero_chunk:
            mass += other[spot]
            other = other.at[spot].set(jnp.where(is_zero, 0.0, other[spot]))
        fresh = plane_inverse(own, other, tables_first, second)
        if chunk == zero_chunk:
            spot = (slice(None), slice(None), 0, 1, 0, 0)
            fresh = fresh.at[spot].set(jnp.where(is_zero, mass, fresh[spot]))
        back.append(exchange(fresh.reshape(devices, count, 2, second, first)))
    updated = depth_inverse(back[:-1], table_of(np.concatenate(inverse[:-1], axis=1)))
    updated = depth_inverse(back[-1:], table_of(inverse[-1]), updated)
    mass = back[zero_chunk][zero_place, 0, 1, 0, 0] * scale
    return updated, mass


def solution(mesh):
    slabs, pencils = mesh.shape["slab"], mesh.shape["pencil"]
    halves = Mesh(mesh.devices.reshape(slabs, 2, pencils // 2), ("slab", "half", "other"))
    field = P("slab", ("half", "other"), None)

    def body(concentration):
        return local(concentration, slabs, pencils // 2)

    return jax.shard_map(
        body, mesh=halves, in_specs=(field,), out_specs=(field, P()), check_vma=False
    )
```
